256 devices in a mesh: row: 16 (over z, core), col: 8 (over y_hi, x), depth: 2 (over y_lo).
Axes of the slice: x: 4, y: 4 (y_hi: 2, y_lo: 2; y = y_hi * 2 + y_lo), z: 8, core: 2. Of those that a mesh axis runs over, the one named last changes fastest.
Arguments:
- a_blocks: float32 [32, 32, 256, 256], P('row', ('depth', 'col')), may hold values from -6 to 6
- a_pattern: int32 [32, 32], P('row', ('depth', 'col')), may hold values from 0 to 1, as said below
- b_blocks: float32 [32, 32, 256, 256], P(('depth', 'row'), 'col'), may hold values from -0.125 to 0.125
- b_pattern: int32 [32, 32], P(('depth', 'row'), 'col'), may hold values from 0 to 1, as said below
- c_pattern: int32 [32, 32], P(('row', 'depth'), 'col'), may hold values 0 or 1
Outputs:
- c_blocks: float32 [32, 32, 256, 256], P(('row', 'depth'), 'col')
The draws below stay inside these ranges and needn't reach their ends.
Inputs may be any that keep to these rules, and one draw needn't show every extreme that they name: Each block row of a_pattern holds between 1 and 8 stored blocks, and some block row holds exactly 8. Each block column of b_pattern holds between 1 and 8 stored blocks, and some block column holds exactly 8.
All inputs are finite; a program needn't handle non-finite values. No bound on the sum of `c_pattern` on one device may be relied on, other than what follows from the above.
Results may differ from the reference program's by a relative error of at most 0.000071.
Values sent between devices are 32-bit elements; how exact they have to be, the bound alone decides.
A program may use at most 128 MiB of HBM per device.

```python
import jax
import jax.numpy as jnp
from jax import lax

BS = 256
NR = 32
NC = 32
NK = 32


def limited_rows(key, rows, cols, most):
    first, second, third = jax.random.split(key, 3)
    scores = jax.random.randint(first, (rows, cols), 0, 1 << 20) * cols + jnp.arange(cols, dtype=jnp.int32)[None, :]
    ranks = jnp.argsort(jnp.argsort(scores, axis=1), axis=1)
    counts = jax.random.randint(second, (rows,), 1, most + 1)
    chosen = jax.random.randint(third, (), 0, rows)
    counts = jnp.where(jnp.arange(rows) == chosen, most, counts)
    return (ranks < counts[:, None]).astype(jnp.int32)


def draw_a_pattern(key, part):
    return limited_rows(jax.random.fold_in(key, 11), NR, NK, NK // 4)


def draw_b_pattern(key, part):
    return limited_rows(jax.random.fold_in(key, 23), NC, NK, NK // 4).T


def with_ends(entries, key, least, high):
    spot = [jax.random.randint(jax.random.fold_in(key, axis), (), 0, length) for axis, length in enumerate(entries.shape)]
    longest = entries.shape.index(max(entries.shape))
    beside = spot[:longest] + [(spot[longest] + 1) % entries.shape[longest]] + spot[longest + 1:]
    return entries.at[tuple(spot)].set(least).at[tuple(beside)].set(high)


def shard_levels(rng, shape, pieces, smallest, top_value):
    loudness, own = 1.0, jax.random.fold_in(rng, 6)
    for position, parts in pieces:
        draws = jnp.exp(jax.random.uniform(jax.random.fold_in(own, position), (parts,), jnp.float32, smallest / len(pieces), top_value / len(pieces)))
        loudness = loudness * jnp.repeat(draws, shape[position] // parts).reshape([-1 if axis == position else 1 for axis in range(len(shape))])
    return loudness


def bell_draw(own_key, dims, spread, most, cuts=(), kind=jnp.bfloat16):
    values = jax.random.normal(own_key, dims, jnp.float32) * spread
    if len(cuts) > 0:
        values = shard_levels(own_key, dims, cuts, -0.22, 0.18) * values
    return jnp.clip(values, min=-most, max=most).astype(kind)


def setup_inputs(seed: int = 0) -> dict:
    key_list = jax.random.split(jax.random.key(seed), 6)
    a_blocks = bell_draw(key_list[0], (NR, NK, BS, BS), 1.0, 6.0, ((0, 16), (1, 16)), jnp.float32)
    a_pattern = draw_a_pattern(jax.random.fold_in(key_list[5], 71), 0)
    b_blocks = bell_draw(key_list[2], (NK, NC, BS, BS), (NK * BS // 4) ** -0.5, 0.125, ((0, 32), (1, 8)), jnp.float32)
    b_pattern = draw_b_pattern(jax.random.fold_in(key_list[5], 71), 0)
    c_pattern = with_ends((jax.random.randint(key_list[4], (NR, NC), 0, 2) < 1).astype(jnp.int32), jax.random.fold_in(key_list[4], 1), 0, 1)
    return {"a_blocks": a_blocks, "a_pattern": a_pattern, "b_blocks": b_blocks, "b_pattern": b_pattern, "c_pattern": c_pattern}


def reference(a_blocks, a_pattern, b_blocks, b_pattern, c_pattern):
    left = a_blocks * a_pattern[:, :, None, None].astype(jnp.float32)
    right = b_blocks * b_pattern[:, :, None, None].astype(jnp.float32)
    product = jnp.einsum("rkab,kcbe->rcae", left, right, precision=lax.Precision.HIGHEST)
    return product * c_pattern[:, :, None, None].astype(jnp.float32)
```

```python
import jax
import jax.numpy as jnp
from jax import lax
from jax.experimental import pallas as pl
from jax.experimental.pallas import tpu as pltpu
from jax.sharding import PartitionSpec as P

MESH = pl.DeviceIdType.MESH
BS = 256
SL = 16
CAP = 8
NSLOT = 2 * CAP
NK = 32


def device(row, col, depth):
    return {"row": row, "col": col, "depth": depth}


def sliced(ref, first, count, piece):
    return ref.at[pl.ds(first, count), pl.ds(pl.multiple_of(piece * SL, SL), SL), :]


def gather_transfers(row, col, depth, a2, b2, a3, b3):
    z, core = lax.div(row, 2), lax.rem(row, 2)
    px = lax.rem(col, 4)
    py = lax.div(col, 4) * 2 + depth

    def plane_id(x, y):
        return lax.rem(y, 2) * 8 + lax.div(y, 2) * 4 + x

    def moved(chunk, first, second):
        dx, dy = (first, second) if chunk == 0 else (second, first)
        return lax.rem(px + (dx + 4), 4), lax.rem(py + (dy + 4), 4)

    def plane_device(chunk, first, second):
        x, y = moved(chunk, first, second)
        return device(row, lax.div(y, 2) * 4 + x, lax.rem(y, 2))

    out = []

    def a_piece(chunk, first, second, lo, count):
        if first == 0 and second == 0:
            return a2.at[pl.ds(chunk * CAP + lo, count)]
        return sliced(a3, chunk * CAP + lo, count, plane_id(*moved(chunk, first, second)))

    def a_target(chunk, first, second, lo, count):
        return sliced(a3, chunk * CAP + lo, count, plane_id(*moved(chunk, first, second)))

    half = {1: 0, -1: CAP // 2}
    for chunk in (0, 1):
        for way in (1, -1):
            key = ("A", chunk, 1, way)
            out.append((key, a_piece(chunk, 0, 0, 0, CAP), a_target(chunk, 0, 0, 0, CAP),
                        plane_device(chunk, way, 0), a_target(chunk, -way, 0, 0, CAP), []))
            out.append((("A", chunk, "1h", way), a_piece(chunk, -way, 0, half[way], CAP // 2),
                        a_target(chunk, -way, 0, half[way], CAP // 2), plane_device(chunk, way, 0),
                        a_target(chunk, 2, 0, half[way], CAP // 2), [key]))
        for first in (0, -1, 1, 2):
            needs = {0: [], -1: [("A", chunk, 1, 1)], 1: [("A", chunk, 1, -1)],
                     2: [("A", chunk, "1h", 1), ("A", chunk, "1h", -1)]}[first]
            for way in (1, -1):
                key = ("A", chunk, 2, first, way)
                out.append((key, a_piece(chunk, first, 0, 0, CAP), a_target(chunk, first, 0, 0, CAP),
                            plane_device(chunk, 0, way), a_target(chunk, first, -way, 0, CAP), needs))
                out.append((("A", chunk, "2h", first, way), a_piece(chunk, first, -way, half[way], CAP // 2),
                            a_target(chunk, first, -way, half[way], CAP // 2), plane_device(chunk, 0, way),
                            a_target(chunk, first, 2, half[way], CAP // 2), [key]))

    def b_id(dz, which):
        return lax.rem(z + (dz + 8), 8) * 2 + which

    def b_piece(chunk, dz):
        if dz == 0:
            return b2.at[pl.ds(chunk * CAP, CAP)]
        return sliced(b3, chunk * CAP, CAP, b_id(dz, core))

    def b_target(chunk, dz, which):
        return sliced(b3, chunk * CAP, CAP, b_id(dz, which))

    for chunk in (0, 1):
        arrived = {0: []}
        for way in (1, -1):
            for hop in range(4):
                if hop == 3 and way != (1, -1)[chunk]:
                    continue
                key = ("B", chunk, way, hop)
                out.append((key, b_piece(chunk, -way * hop), b_target(chunk, -way * hop, core),
                            device(b_id(way, core), col, depth), b_target(chunk, -way * (hop + 1), core),
                            [("B", chunk, way, hop - 1)] if hop else []))
                arrived[-way * (hop + 1)] = [key]
        for dz, needs in arrived.items():
            out.append((("S", chunk, dz), b_piece(chunk, dz), b_target(chunk, dz, core),
                        device(z * 2 + 1 - core, col, depth), b_target(chunk, dz, 1 - core), needs))
    return out


def in_level_order(transfers):
    by_key = {t[0]: t for t in transfers}

    def level(key):
        return 1 + max([level(k) for k in by_key[key][5]], default=0)

    return sorted(transfers, key=lambda t: level(t[0]))


NXFER = 70


def exchange_kernel(ap_ref, bp_ref, a_ref, b_ref, a3, b3, pout,
                    a1, b1, pa, pb, my_pa, my_pb, ra, rb, a2, b2,
                    sa, xa, spa, xpa, sb, xb, spb, xpb, own_sem, ring_s, ring_x):
    row, col, depth = lax.axis_index("row"), lax.axis_index("col"), lax.axis_index("depth")
    me_a = depth * 8 + col
    me_b = depth * 16 + row

    def plane(i):
        return device(row, lax.rem(i, 8), lax.div(i, 8))

    def group(i):
        return device(lax.rem(i, 16), col, lax.div(i, 16))

    barrier = pltpu.get_barrier_semaphore()

    @pl.loop(1, 16)
    def _(o):
        pl.semaphore_signal(barrier, inc=1, device_id=plane(lax.rem(me_a + o, 16)), device_id_type=MESH)

    @pl.loop(1, 32)
    def _(o):
        pl.semaphore_signal(barrier, inc=1, device_id=group(lax.rem(me_b + o, 32)), device_id_type=MESH)

    for i in range(2):
        for j in range(2):
            my_pa[i, j] = jnp.full((8, 128), ap_ref[i, j], jnp.int32)
            my_pb[i, j] = jnp.full((8, 128), bp_ref[0, 2 * i + j], jnp.int32)
    pa[me_a] = my_pa[...]
    pb[me_b] = my_pb[depth]
    own_a = pltpu.make_async_copy(a_ref.at[:, :, pl.ds(pl.multiple_of(me_a * SL, SL), SL), :], a1.at[me_a], own_sem.at[0])
    own_b = pltpu.make_async_copy(
        b_ref.at[0, pl.ds(2 * depth, 2), pl.ds(pl.multiple_of(row * SL, SL), SL), :], b1.at[me_b], own_sem.at[1])
    own_a.start()
    own_b.start()
    pl.semaphore_wait(barrier, 46)

    def copy_a(to, frm):
        return pltpu.make_async_remote_copy(
            src_ref=a_ref.at[:, :, pl.ds(pl.multiple_of(to * SL, SL), SL), :], dst_ref=a1.at[frm],
            send_sem=sa.at[to], recv_sem=xa.at[frm], device_id=plane(to), device_id_type=MESH)

    def copy_pa(to, frm):
        return pltpu.make_async_remote_copy(
            src_ref=my_pa, dst_ref=pa.at[frm],
            send_sem=spa.at[to], recv_sem=xpa.at[frm], device_id=plane(to), device_id_type=MESH)

    def copy_b(to, frm):
        return pltpu.make_async_remote_copy(
            src_ref=b_ref.at[0, pl.ds(2 * lax.div(to, 16), 2), pl.ds(pl.multiple_of(lax.rem(to, 16) * SL, SL), SL), :],
            dst_ref=b1.at[frm], send_sem=sb.at[to], recv_sem=xb.at[frm], device_id=group(to), device_id_type=MESH)

    def copy_pb(to, frm):
        return pltpu.make_async_remote_copy(
            src_ref=my_pb.at[lax.div(to, 16)], dst_ref=pb.at[frm],
            send_sem=spb.at[to], recv_sem=xpb.at[frm], device_id=group(to), device_id_type=MESH)

    @pl.loop(1, 32)
    def _(o):
        to = lax.rem(me_b + o, 32)
        copy_pb(to, me_b).start()
        copy_b(to, me_b).start()

    @pl.loop(1, 16)
    def _(o):
        to = lax.rem(me_a + o, 16)
        copy_pa(to, me_a).start()
        copy_a(to, me_a).start()

    @pl.loop(1, 16)
    def _(o):
        frm = lax.rem(me_a + 16 - o, 16)
        copy_pa(frm, frm).wait_recv()
        copy_a(frm, frm).wait_recv()

    own_a.wait()
    lanes = lax.broadcasted_iota(jnp.int32, (8, 128), 1)
    zero = jnp.zeros((8, 128), jnp.int32)

    def rank(ranks, g, k, p, carry):
        before, listed = carry
        ranks[g, k] = jnp.where(p > 0, before, -1)
        return before + p, jnp.where(lanes == k, p, listed)

    def rank_a(s, carry):
        for j in range(2):
            carry = tuple(rank(ra, g, 2 * s + j, pa[s, g, j], carry[g]) for g in range(2))
        return carry

    done = lax.fori_loop(0, 16, rank_a, ((zero, zero), (zero, zero)))
    pout[0] = done[0][1]
    pout[1] = done[1][1]

    def pick(ranks, load, dst, slot):
        g, j = lax.div(slot, CAP), lax.rem(slot, CAP)
        acc = [jnp.zeros((8, 128), jnp.float32)] * 4
        for k in range(NK):
            here = ranks[g, k] == j
            acc = [jnp.where(here, load(g, k, q), acc[q]) for q in range(4)]
        for q in range(4):
            dst[slot, pl.ds(8 * (q // 2), 8), pl.ds(128 * (q % 2), 128)] = acc[q]

    @pl.loop(0, NSLOT)
    def _(slot):
        pick(ra, lambda g, k, q: a1[k // 2, g, k % 2, pl.ds(8 * (q // 2), 8), pl.ds(128 * (q % 2), 128)], a2, slot)

    transfers = in_level_order(gather_transfers(row, col, depth, a2, b2, a3, b3))
    index = {t[0]: i for i, t in enumerate(transfers)}
    made = {}
    for key, src, dst, dev, arrives, needs in transfers:
        i = index[key]
        send = pltpu.make_async_remote_copy(src_ref=src, dst_ref=dst, send_sem=ring_s.at[i], recv_sem=ring_x.at[i],
                                            device_id=dev, device_id_type=MESH)
        recv = pltpu.make_async_remote_copy(src_ref=arrives, dst_ref=arrives, send_sem=ring_s.at[i],
                                            recv_sem=ring_x.at[i], device_id=dev, device_id_type=MESH)
        made[key] = (send, recv)
    arrived = set()

    def start(t):
        for need in t[5]:
            if need not in arrived:
                made[need][1].wait_recv()
                arrived.add(need)
        made[t[0]][0].start()

    put_a = pltpu.make_async_copy(a2, sliced(a3, 0, NSLOT, me_a), own_sem.at[2])
    put_a.start()
    first_a = [t for t in transfers if t[0][0] == "A" and not t[5]]
    for t in first_a:
        start(t)

    @pl.loop(1, 32)
    def _(o):
        frm = lax.rem(me_b + 32 - o, 32)
        copy_pb(frm, frm).wait_recv()
        copy_b(frm, frm).wait_recv()

    own_b.wait()

    def rank_b(k, carry):
        return tuple(rank(rb, g, k, pb[k, g], carry[g]) for g in range(2))

    done = lax.fori_loop(0, NK, rank_b, ((zero, zero), (zero, zero)))
    pout[2] = done[0][1]
    pout[3] = done[1][1]

    @pl.loop(0, NSLOT)
    def _(slot):
        pick(rb, lambda g, k, q: b1[k, g, pl.ds(8 * (q // 2), 8), pl.ds(128 * (q % 2), 128)], b2, slot)

    put_b = pltpu.make_async_copy(b2, sliced(b3, 0, NSLOT, row), own_sem.at[3])
    put_b.start()
    for t in transfers:
        if t not in first_a:
            start(t)
    for t in transfers:
        if t[0] not in arrived:
            made[t[0]][1].wait_recv()
    for t in transfers:
        made[t[0]][0].wait_send()
    put_a.wait()
    put_b.wait()

    @pl.loop(1, 32)
    def _(o):
        to = lax.rem(me_b + o, 32)
        copy_pb(to, me_b).wait_send()
        copy_b(to, me_b).wait_send()

    @pl.loop(1, 16)
    def _(o):
        to = lax.rem(me_a + o, 16)
        copy_pa(to, me_a).wait_send()
        copy_a(to, me_a).wait_send()


def exchange(a_pattern, b_pattern, a_blocks, b_blocks):
    any_spec = pl.BlockSpec(memory_space=pl.ANY)
    smem = pl.BlockSpec(memory_space=pltpu.SMEM)
    dma = pltpu.SemaphoreType.DMA
    f32, i32 = jnp.float32, jnp.int32
    return pl.pallas_call(
        exchange_kernel,
        out_shape=(jax.ShapeDtypeStruct((NSLOT, BS, BS), f32), jax.ShapeDtypeStruct((NSLOT, BS, BS), f32),
                   jax.ShapeDtypeStruct((4, 8, 128), i32)),
        in_specs=[smem, smem, any_spec, any_spec],
        out_specs=(any_spec, any_spec, pl.BlockSpec(memory_space=pltpu.VMEM)),
        scratch_shapes=[
            pltpu.VMEM((16, 2, 2, SL, BS), f32), pltpu.VMEM((NK, 2, SL, BS), f32),
            pltpu.VMEM((16, 2, 2, 8, 128), i32), pltpu.VMEM((NK, 2, 8, 128), i32),
            pltpu.VMEM((2, 2, 8, 128), i32), pltpu.VMEM((2, 2, 8, 128), i32),
            pltpu.VMEM((2, NK, 8, 128), i32), pltpu.VMEM((2, NK, 8, 128), i32),
            pltpu.VMEM((NSLOT, SL, BS), f32), pltpu.VMEM((NSLOT, SL, BS), f32),
            dma((16,)), dma((16,)), dma((16,)), dma((16,)),
            dma((32,)), dma((32,)), dma((32,)), dma((32,)),
            dma((4,)), dma((NXFER,)), dma((NXFER,)),
        ],
        compiler_params=pltpu.CompilerParams(collective_id=0, has_side_effects=True),
        name="exchange",
    )(a_pattern, b_pattern, a_blocks, b_blocks)


def product_kernel(p_ref, a3, b3, out):
    for g in range(2):
        for c in range(2):
            out[g, c] = jnp.zeros((BS, BS), jnp.float32)

            def step(k, carry, g=g, c=c):
                ia, ib = carry
                ha, hb = p_ref[g, 0, k], p_ref[2 + c, 0, k]

                @pl.when(ha * hb > 0)
                def _():
                    out[g, c] += jnp.dot(a3[g * CAP + ia], b3[c * CAP + ib], precision=lax.Precision.HIGHEST,
                                         preferred_element_type=jnp.float32)

                return ia + ha, ib + hb

            lax.fori_loop(0, NK, step, (0, 0))


def product(pout, a3, b3):
    vmem = pl.BlockSpec(memory_space=pltpu.VMEM)
    return pl.pallas_call(
        product_kernel,
        out_shape=jax.ShapeDtypeStruct((2, 2, BS, BS), jnp.float32),
        in_specs=[pl.BlockSpec(memory_space=pltpu.SMEM), vmem, vmem],
        out_specs=vmem,
        name="product",
    )(pout, a3, b3)


def swap_kernel(part, out, sems):
    row, col, depth = lax.axis_index("row"), lax.axis_index("col"), lax.axis_index("depth")
    other = device(row, col, 1 - depth)
    barrier = pltpu.get_barrier_semaphore()
    pl.semaphore_signal(barrier, inc=1, device_id=other, device_id_type=MESH)
    keep = pltpu.make_async_copy(part.at[depth], out.at[pl.ds(2 * depth, 2)], sems.at[0])
    keep.start()
    pl.semaphore_wait(barrier, 1)
    send = pltpu.make_async_remote_copy(src_ref=part.at[1 - depth], dst_ref=out.at[pl.ds(2 * depth, 2)],
                                        send_sem=sems.at[1], recv_sem=sems.at[2], device_id=other, device_id_type=MESH)
    recv = pltpu.make_async_remote_copy(src_ref=part.at[1 - depth], dst_ref=out.at[pl.ds(2 - 2 * depth, 2)],
                                        send_sem=sems.at[1], recv_sem=sems.at[2], device_id=other, device_id_type=MESH)
    send.start()
    keep.wait()
    recv.wait_recv()
    send.wait_send()


def swap(part):
    return pl.pallas_call(
        swap_kernel,
        out_shape=jax.ShapeDtypeStruct((4, BS, BS), jnp.float32),
        in_specs=[pl.BlockSpec(memory_space=pltpu.VMEM)],
        out_specs=pl.BlockSpec(memory_space=pl.ANY),
        scratch_shapes=[pltpu.SemaphoreType.DMA((3,))],
        compiler_params=pltpu.CompilerParams(collective_id=1, has_side_effects=True),
        name="swap",
    )(part)


def local(a_blocks, a_pattern, b_blocks, b_pattern, c_pattern):
    a3, b3, pout = exchange(a_pattern, b_pattern, a_blocks, b_blocks)
    c = swap(product(pout, a3, b3))
    return (c * c_pattern[0][:, None, None].astype(jnp.float32))[None]


def solution(mesh):
    in_specs = (
        P("row", ("depth", "col"), None, None),
        P("row", ("depth", "col")),
        P(("depth", "row"), "col", None, None),
        P(("depth", "row"), "col"),
        P(("row", "depth"), "col"),
    )
    out_specs = P(("row", "depth"), "col", None, None)
    return jax.shard_map(local, mesh=mesh, in_specs=in_specs, out_specs=out_specs, check_vma=False)
```

```python
import jax
import jax.numpy as jnp
from jax import lax
from jax.experimental import pallas as pl
from jax.experimental.pallas import tpu as pltpu
from jax.sharding import PartitionSpec as P

MESH = pl.DeviceIdType.MESH
BS = 256
SL = 16
CAP = 8
NSLOT = 2 * CAP
NK = 32


def device(row, col, depth):
    return {"row": row, "col": col, "depth": depth}


def sliced(ref, first, count, piece):
    return ref.at[pl.ds(first, count), pl.ds(pl.multiple_of(piece * SL, SL), SL), :]


def gather_transfers(row, col, depth, a2, b2, a3, b3):
    z, core = lax.div(row, 2), lax.rem(row, 2)
    px = lax.rem(col, 4)
    py = lax.div(col, 4) * 2 + depth

    def plane_id(x, y):
        return lax.rem(y, 2) * 8 + lax.div(y, 2) * 4 + x

    def moved(chunk, first, second):
        dx, dy = (first, second) if chunk == 0 else (second, first)
        return lax.rem(px + (dx + 4), 4), lax.rem(py + (dy + 4), 4)

    def plane_device(chunk, first, second):
        x, y = moved(chunk, first, second)
        return device(row, lax.div(y, 2) * 4 + x, lax.rem(y, 2))

    out = []

    def a_piece(chunk, first, second, lo, count):
        if first == 0 and second == 0:
            return a2.at[pl.ds(chunk * CAP + lo, count)]
        return sliced(a3, chunk * CAP + lo, count, plane_id(*moved(chunk, first, second)))

    def a_target(chunk, first, second, lo, count):
        return sliced(a3, chunk * CAP + lo, count, plane_id(*moved(chunk, first, second)))

    half = {1: 0, -1: CAP // 2}
    for chunk in (0, 1):
        for way in (1, -1):
            key = ("A", chunk, 1, way)
            out.append((key, a_piece(chunk, 0, 0, 0, CAP), a_target(chunk, 0, 0, 0, CAP),
                        plane_device(chunk, way, 0), a_target(chunk, -way, 0, 0, CAP), []))
            out.append((("A", chunk, "1h", way), a_piece(chunk, -way, 0, half[way], CAP // 2),
                        a_target(chunk, -way, 0, half[way], CAP // 2), plane_device(chunk, way, 0),
                        a_target(chunk, 2, 0, half[way], CAP // 2), [key]))
        for first in (0, -1, 1, 2):
            needs = {0: [], -1: [("A", chunk, 1, 1)], 1: [("A", chunk, 1, -1)],
                     2: [("A", chunk, "1h", 1), ("A", chunk, "1h", -1)]}[first]
            for way in (1, -1):
                key = ("A", chunk, 2, first, way)
                out.append((key, a_piece(chunk, first, 0, 0, CAP), a_target(chunk, first, 0, 0, CAP),
                            plane_device(chunk, 0, way), a_target(chunk, first, -way, 0, CAP), needs))
                out.append((("A", chunk, "2h", first, way), a_piece(chunk, first, -way, half[way], CAP // 2),
                            a_target(chunk, first, -way, half[way], CAP // 2), plane_device(chunk, 0, way),
                            a_target(chunk, first, 2, half[way], CAP // 2), [key]))

    def b_id(dz, which):
        return lax.rem(z + (dz + 8), 8) * 2 + which

    def b_piece(chunk, dz):
        if dz == 0:
            return b2.at[pl.ds(chunk * CAP, CAP)]
        return sliced(b3[chunk], 0, CAP, b_id(dz, core))

    def b_target(chunk, dz, which):
        return sliced(b3[chunk], 0, CAP, b_id(dz, which))

    for chunk in (0, 1):
        arrived = {0: []}
        for way in (1, -1):
            for hop in range(4):
                if hop == 3 and way != (1, -1)[chunk]:
                    continue
                key = ("B", chunk, way, hop)
                out.append((key, b_piece(chunk, -way * hop), b_target(chunk, -way * hop, core),
                            device(b_id(way, core), col, depth), b_target(chunk, -way * (hop + 1), core),
                            [("B", chunk, way, hop - 1)] if hop else []))
                arrived[-way * (hop + 1)] = [key]
        for dz, needs in arrived.items():
            out.append((("S", chunk, dz), b_piece(chunk, dz), b_target(chunk, dz, core),
                        device(z * 2 + 1 - core, col, depth), b_target(chunk, dz, 1 - core), needs))
    return out


NXFER = 70


def start_time(key):
    if key[0] == "A":
        level = {1: 0, "1h": 1}.get(key[2])
        if level is None:
            level = {0: 0, -1: 1, 1: 1, 2: 2}[key[3]] + (1 if key[2] == "2h" else 0)
        return 30 + 6 * level
    first, each = ((24, 4.5), (35, 4.5))[key[1]]
    if key[0] == "B":
        return first + each * key[3]
    return first + each * abs(key[2]) + 0.1


def kernel(ap_ref, bp_ref, a_ref, b_ref, out,
           a1, b1, pa, pb, my_pa, my_pb, ra, rb, a2, b2, a3, b3_0, b3_1, c_own, c_other, match, match_s,
           sa, xa, spa, xpa, sb, xb, spb, xpb, own_sem, ring_s, ring_x, swap_s, swap_x):
    row, col, depth = lax.axis_index("row"), lax.axis_index("col"), lax.axis_index("depth")
    b3 = (b3_0, b3_1)
    me_a = depth * 8 + col
    me_b = depth * 16 + row

    def plane(i):
        return device(row, lax.rem(i, 8), lax.div(i, 8))

    def group(i):
        return device(lax.rem(i, 16), col, lax.div(i, 16))

    def piece(i):
        return pl.ds(pl.multiple_of(i * SL, SL), SL)

    barrier = pltpu.get_barrier_semaphore()

    @pl.loop(1, 16)
    def _(o):
        pl.semaphore_signal(barrier, inc=1, device_id=plane(lax.rem(me_a + o, 16)), device_id_type=MESH)

    @pl.loop(1, 32)
    def _(o):
        pl.semaphore_signal(barrier, inc=1, device_id=group(lax.rem(me_b + o, 32)), device_id_type=MESH)

    for i in range(2):
        for j in range(2):
            my_pa[i, j] = jnp.full((1, 128), ap_ref[i, j], jnp.int32)
            my_pb[i, j] = jnp.full((1, 128), bp_ref[0, 2 * i + j], jnp.int32)
    pa[me_a] = my_pa[...]
    pb[me_b] = my_pb[depth]
    own = [
        pltpu.make_async_copy(a_ref.at[:, :, piece(me_a), :], a1.at[me_a], own_sem.at[0]),
        pltpu.make_async_copy(b_ref.at[0, 2 * depth, piece(row), :], b1.at[0, me_b], own_sem.at[1]),
        pltpu.make_async_copy(b_ref.at[0, 2 * depth + 1, piece(row), :], b1.at[1, me_b], own_sem.at[2]),
    ]
    for copy in own:
        copy.start()
    pl.semaphore_wait(barrier, 46)

    def copy_a(to, frm):
        return pltpu.make_async_remote_copy(
            src_ref=a_ref.at[:, :, piece(to), :], dst_ref=a1.at[frm],
            send_sem=sa.at[to], recv_sem=xa.at[frm], device_id=plane(to), device_id_type=MESH)

    def copy_pa(to, frm):
        return pltpu.make_async_remote_copy(
            src_ref=my_pa, dst_ref=pa.at[frm],
            send_sem=spa.at[to], recv_sem=xpa.at[frm], device_id=plane(to), device_id_type=MESH)

    def copy_b(c, to, frm):
        return pltpu.make_async_remote_copy(
            src_ref=b_ref.at[0, 2 * lax.div(to, 16) + c, piece(lax.rem(to, 16)), :], dst_ref=b1.at[c, frm],
            send_sem=sb.at[c, to], recv_sem=xb.at[c, frm], device_id=group(to), device_id_type=MESH)

    def copy_pb(to, frm):
        return pltpu.make_async_remote_copy(
            src_ref=my_pb.at[lax.div(to, 16)], dst_ref=pb.at[frm],
            send_sem=spb.at[to], recv_sem=xpb.at[frm], device_id=group(to), device_id_type=MESH)

    @pl.loop(1, 32)
    def _(o):
        to = lax.rem(me_b + o, 32)
        copy_pb(to, me_b).start()
        copy_b(0, to, me_b).start()

    @pl.loop(1, 16)
    def _(o):
        to = lax.rem(me_a + o, 16)
        copy_pa(to, me_a).start()
        copy_a(to, me_a).start()

    @pl.loop(1, 32)
    def _(o):
        copy_b(1, lax.rem(me_b + o, 32), me_b).start()

    zero = jnp.zeros((8, 128), jnp.int32)

    def rank(ranks, g, k, p, before):
        p = jnp.broadcast_to(p, (8, 128))
        ranks[g, k] = jnp.where(p > 0, before, -1)
        return before + p

    @pl.loop(1, 32)
    def _(o):
        frm = lax.rem(me_b + 32 - o, 32)
        copy_pb(frm, frm).wait_recv()

    def rank_b(k, carry):
        return tuple(rank(rb, g, k, pb[k, g], carry[g]) for g in range(2))

    lax.fori_loop(0, NK, rank_b, (zero, zero))

    @pl.loop(1, 16)
    def _(o):
        frm = lax.rem(me_a + 16 - o, 16)
        copy_pa(frm, frm).wait_recv()

    def rank_a(s, carry):
        for j in range(2):
            carry = tuple(rank(ra, g, 2 * s + j, pa[s, g, j], carry[g]) for g in range(2))
        return carry

    lax.fori_loop(0, 16, rank_a, (zero, zero))

    lanes = lax.broadcasted_iota(jnp.int32, (8, 128), 1)
    for g in range(2):
        def meet(k, carry, g=g):
            ours = ra[g, k]
            return tuple(jnp.where(lanes == ours, rb[c, k] + 1, carry[c]) for c in range(2))

        met = lax.fori_loop(0, NK, meet, (zero, zero))
        for c in range(2):
            match[g, c] = met[c]

    def pick(ranks, load, dst, slot):
        g, j = lax.div(slot, CAP), lax.rem(slot, CAP)
        acc = [jnp.zeros((8, 128), jnp.float32)] * 4
        for k in range(NK):
            here = ranks[g, k] == j
            acc = [jnp.where(here, load(g, k, q), acc[q]) for q in range(4)]
        for q in range(4):
            dst[slot, pl.ds(8 * (q // 2), 8), pl.ds(128 * (q % 2), 128)] = acc[q]

    def tile(q):
        return pl.ds(8 * (q // 2), 8), pl.ds(128 * (q % 2), 128)

    puts = []

    def pack_a():
        @pl.loop(1, 16)
        def _(o):
            frm = lax.rem(me_a + 16 - o, 16)
            copy_a(frm, frm).wait_recv()

        own[0].wait()

        @pl.loop(0, NSLOT)
        def _(slot):
            pick(ra, lambda g, k, q: a1[(k // 2, g, k % 2, *tile(q))], a2, slot)

        put = pltpu.make_async_copy(a2, sliced(a3, 0, NSLOT, me_a), own_sem.at[3])
        put.start()
        puts.append(put)

    def pack_b(c):
        @pl.loop(1, 32)
        def _(o):
            frm = lax.rem(me_b + 32 - o, 32)
            copy_b(c, frm, frm).wait_recv()

        own[1 + c].wait()

        @pl.loop(c * CAP, (c + 1) * CAP)
        def _(slot):
            pick(rb, lambda g, k, q: b1[(c, k, *tile(q))], b2, slot)

        put = pltpu.make_async_copy(b2.at[pl.ds(c * CAP, CAP)], sliced(b3[c], 0, CAP, row), own_sem.at[4 + c])
        put.start()
        puts.append(put)

    transfers = gather_transfers(row, col, depth, a2, b2, a3, b3)
    assert len(transfers) == NXFER
    made = {}
    for i, (key, src, dst, dev, arrives, needs) in enumerate(transfers):
        made[key] = tuple(
            pltpu.make_async_remote_copy(src_ref=a, dst_ref=b, send_sem=ring_s.at[i], recv_sem=ring_x.at[i],
                                         device_id=dev, device_id_type=MESH)
            for a, b in ((src, dst), (arrives, arrives)))
    arrived = set()

    def wait_for(keys):
        for key in keys:
            if key not in arrived:
                made[key][1].wait_recv()
                arrived.add(key)

    smem_copy = pltpu.make_async_copy(match, match_s, own_sem.at[6])
    smem_copy.start()
    packs = [(23.9, lambda: pack_b(0)), (29.9, pack_a), (34.9, lambda: pack_b(1))]
    for key, src, dst, dev, arrives, needs in sorted(transfers, key=lambda t: start_time(t[0])):
        while packs and packs[0][0] < start_time(key):
            packs.pop(0)[1]()
        wait_for(needs)
        made[key][0].start()

    wait_for([t[0] for t in transfers if t[0][0] == "A"])
    puts[1].wait()
    smem_copy.wait()

    def split(x):
        high = x.astype(jnp.bfloat16)
        return high, (x - high.astype(jnp.float32)).astype(jnp.bfloat16)

    def block(g, c, dst):
        dst[c] = jnp.zeros((BS, BS), jnp.float32)

        @pl.loop(0, CAP)
        def _(j):
            slot = match_s[g, c, 0, j]
            weight = jnp.where(slot > 0, 1.0, 0.0).astype(jnp.float32)
            ah, al = split(a3[g * CAP + j])
            bh, bl = split(b3[c][jnp.maximum(slot - 1, 0)])
            left = jnp.concatenate([ah, ah, al], axis=1)
            right = jnp.concatenate([bh, bl, bh], axis=0)
            dst[c] += weight * jnp.dot(left, right, preferred_element_type=jnp.float32)

    other = device(row, col, 1 - depth)

    def swap(c, d):
        return pltpu.make_async_remote_copy(src_ref=c_other.at[c], dst_ref=out.at[2 * d + c], send_sem=swap_s.at[c],
                                            recv_sem=swap_x.at[c], device_id=other, device_id_type=MESH)

    keeps = []
    for c in range(2):
        wait_for([t[0] for t in transfers if t[0][0] in "BS" and t[0][1] == c])
        puts[2 * c].wait()
        block(1 - depth, c, c_other)
        swap(c, depth).start()
        block(depth, c, c_own)
        keep = pltpu.make_async_copy(c_own.at[c], out.at[2 * depth + c], own_sem.at[7 + c])
        keep.start()
        keeps.append(keep)

    for t in transfers:
        made[t[0]][0].wait_send()

    @pl.loop(1, 32)
    def _(o):
        to = lax.rem(me_b + o, 32)
        copy_pb(to, me_b).wait_send()
        copy_b(0, to, me_b).wait_send()
        copy_b(1, to, me_b).wait_send()

    @pl.loop(1, 16)
    def _(o):
        to = lax.rem(me_a + o, 16)
        copy_pa(to, me_a).wait_send()
        copy_a(to, me_a).wait_send()

    for c in range(2):
        keeps[c].wait()
        swap(c, 1 - depth).wait_recv()
        swap(c, depth).wait_send()


def multiply(a_pattern, b_pattern, a_blocks, b_blocks):
    any_spec = pl.BlockSpec(memory_space=pl.ANY)
    smem = pl.BlockSpec(memory_space=pltpu.SMEM)
    dma = pltpu.SemaphoreType.DMA
    f32, i32 = jnp.float32, jnp.int32
    return pl.pallas_call(
        kernel,
        out_shape=jax.ShapeDtypeStruct((4, BS, BS), f32),
        in_specs=[smem, smem, any_spec, any_spec],
        out_specs=any_spec,
        scratch_shapes=[
            pltpu.VMEM((16, 2, 2, SL, BS), f32), pltpu.VMEM((2, NK, SL, BS), f32),
            pltpu.VMEM((16, 2, 2, 1, 128), i32), pltpu.VMEM((NK, 2, 1, 128), i32),
            pltpu.VMEM((2, 2, 1, 128), i32), pltpu.VMEM((2, 2, 1, 128), i32),
            pltpu.VMEM((2, NK, 8, 128), i32), pltpu.VMEM((2, NK, 8, 128), i32),
            pltpu.VMEM((NSLOT, SL, BS), f32), pltpu.VMEM((NSLOT, SL, BS), f32),
            pltpu.VMEM((NSLOT, BS, BS), f32), pltpu.VMEM((CAP, BS, BS), f32), pltpu.VMEM((CAP, BS, BS), f32),
            pltpu.VMEM((2, BS, BS), f32), pltpu.VMEM((2, BS, BS), f32),
            pltpu.VMEM((2, 2, 8, 128), i32), pltpu.SMEM((2, 2, 8, 128), i32),
            dma((16,)), dma((16,)), dma((16,)), dma((16,)),
            dma((2, 32)), dma((2, 32)), dma((32,)), dma((32,)),
            dma((9,)), dma((NXFER,)), dma((NXFER,)), dma((2,)), dma((2,)),
        ],
        compiler_params=pltpu.CompilerParams(collective_id=0, has_side_effects=True),
        name="multiply",
    )(a_pattern, b_pattern, a_blocks, b_blocks)


def local(a_blocks, a_pattern, b_blocks, b_pattern, c_pattern):
    c = multiply(a_pattern, b_pattern, a_blocks, b_blocks)
    return (c * c_pattern[0][:, None, None].astype(jnp.float32))[None]


def solution(mesh):
    in_specs = (
        P("row", ("depth", "col"), None, None),
        P("row", ("depth", "col")),
        P(("depth", "row"), "col", None, None),
        P(("depth", "row"), "col"),
        P(("row", "depth"), "col"),
    )
    out_specs = P(("row", "depth"), "col", None, None)
    return jax.shard_map(local, mesh=mesh, in_specs=in_specs, out_specs=out_specs, check_vma=False)
```

```python
import functools

import jax
import jax.numpy as jnp
from jax import lax
from jax.experimental import pallas as pl
from jax.experimental.pallas import tpu as pltpu
from jax.sharding import PartitionSpec as P

MESH = pl.DeviceIdType.MESH
BS = 256
SL = 16
CAP = 8
NSLOT = 2 * CAP
NK = 32
A_CHUNKS = ((0, 8, "yx"), (8, 8, "xy"))
B_CHUNKS = ((0, 0, 4, 1), (0, 4, 4, -1), (1, 0, 4, 1), (1, 4, 4, -1))
NXFER = 20 * len(A_CHUNKS) + 15 * len(B_CHUNKS)


def device(row, col, depth):
    return {"row": row, "col": col, "depth": depth}


def sliced(ref, first, count, piece):
    return ref.at[pl.ds(first, count), pl.ds(pl.multiple_of(piece * SL, SL), SL), :]


def gather_transfers(row, col, depth, a2, b2, a3, b3):
    z, core = lax.div(row, 2), lax.rem(row, 2)
    px = lax.rem(col, 4)
    py = lax.div(col, 4) * 2 + depth

    def plane_id(x, y):
        return lax.rem(y, 2) * 8 + lax.div(y, 2) * 4 + x

    def moved(chunk, first, second):
        dx, dy = (first, second) if A_CHUNKS[chunk][2] == "xy" else (second, first)
        return lax.rem(px + (dx + 4), 4), lax.rem(py + (dy + 4), 4)

    def plane_device(chunk, first, second):
        x, y = moved(chunk, first, second)
        return device(row, lax.div(y, 2) * 4 + x, lax.rem(y, 2))

    out = []

    def a_piece(chunk, first, second, lo, count):
        if first == 0 and second == 0:
            return a2.at[pl.ds(lo, count)]
        return sliced(a3, lo, count, plane_id(*moved(chunk, first, second)))

    def a_target(chunk, first, second, lo, count):
        return sliced(a3, lo, count, plane_id(*moved(chunk, first, second)))

    for chunk in range(len(A_CHUNKS)):
        lo, count, _ = A_CHUNKS[chunk]
        half = {1: lo, -1: lo + count // 2}
        for way in (1, -1):
            key = ("A", chunk, 1, way)
            out.append((key, a_piece(chunk, 0, 0, lo, count), a_target(chunk, 0, 0, lo, count),
                        plane_device(chunk, way, 0), a_target(chunk, -way, 0, lo, count), []))
            out.append((("A", chunk, "1h", way), a_piece(chunk, -way, 0, half[way], count // 2),
                        a_target(chunk, -way, 0, half[way], count // 2), plane_device(chunk, way, 0),
                        a_target(chunk, 2, 0, half[way], count // 2), [key]))
        for first in (0, -1, 1, 2):
            needs = {0: [], -1: [("A", chunk, 1, 1)], 1: [("A", chunk, 1, -1)],
                     2: [("A", chunk, "1h", 1), ("A", chunk, "1h", -1)]}[first]
            for way in (1, -1):
                key = ("A", chunk, 2, first, way)
                out.append((key, a_piece(chunk, first, 0, lo, count), a_target(chunk, first, 0, lo, count),
                            plane_device(chunk, 0, way), a_target(chunk, first, -way, lo, count), needs))
                out.append((("A", chunk, "2h", first, way), a_piece(chunk, first, -way, half[way], count // 2),
                            a_target(chunk, first, -way, half[way], count // 2), plane_device(chunk, 0, way),
                            a_target(chunk, first, 2, half[way], count // 2), [key]))

    def b_id(dz, which):
        return lax.rem(z + (dz + 8), 8) * 2 + which

    def b_piece(chunk, dz):
        c, lo, count, _ = B_CHUNKS[chunk]
        if dz == 0:
            return b2.at[pl.ds(c * CAP + lo, count)]
        return sliced(b3[c], lo, count, b_id(dz, core))

    def b_target(chunk, dz, which):
        c, lo, count, _ = B_CHUNKS[chunk]
        return sliced(b3[c], lo, count, b_id(dz, which))

    for chunk in range(len(B_CHUNKS)):
        arrived = {0: []}
        for way in (1, -1):
            for hop in range(4):
                if hop == 3 and way != B_CHUNKS[chunk][3]:
                    continue
                key = ("B", chunk, way, hop)
                out.append((key, b_piece(chunk, -way * hop), b_target(chunk, -way * hop, core),
                            device(b_id(way, core), col, depth), b_target(chunk, -way * (hop + 1), core),
                            [("B", chunk, way, hop - 1)] if hop else []))
                arrived[-way * (hop + 1)] = [key]
        for dz, needs in arrived.items():
            out.append((("S", chunk, dz), b_piece(chunk, dz), b_target(chunk, dz, core),
                        device(z * 2 + 1 - core, col, depth), b_target(chunk, dz, 1 - core), needs))
    return out


def start_time(key):
    if key[0] == "A":
        level = {1: 0, "1h": 1}.get(key[2])
        if level is None:
            level = {0: 0, -1: 1, 1: 1, 2: 2}[key[3]] + (1 if key[2] == "2h" else 0)
        return 38.5 + 0.3 * key[1] + 8.6 * level
    c, lo = B_CHUNKS[key[1]][:2]
    times = ((36, 42.6, 49.2, 55.8), (45, 49.8, 54.6, 59.4))[c]
    if key[0] == "B":
        return times[key[3]] + 1.3 * lo / 4
    return times[min(abs(key[2]), 3)] + 1.3 * lo / 4 + (0.1 if abs(key[2]) < 4 else 4.5)


def kernel(ap_ref, bp_ref, a_ref, b_ref, out,
           a1, b1, pa, pb, my_pa, my_pb, ra, rb, a2, b2, a3, b3_0, b3_1, c_own, c_other, match, match_s,
           sa, xa, spa, xpa, sb, xb, spb, xpb, own_sem, ring_s, ring_x, swap_s, swap_x):
    row, col, depth = lax.axis_index("row"), lax.axis_index("col"), lax.axis_index("depth")
    b3 = (b3_0, b3_1)
    me_a = depth * 8 + col
    me_b = depth * 16 + row

    def plane(i):
        return device(row, lax.rem(i, 8), lax.div(i, 8))

    def group(i):
        return device(lax.rem(i, 16), col, lax.div(i, 16))

    def piece(i):
        return pl.ds(pl.multiple_of(i * SL, SL), SL)

    barrier = pltpu.get_barrier_semaphore()

    @pl.loop(1, 16)
    def _(o):
        pl.semaphore_signal(barrier, inc=1, device_id=plane(lax.rem(me_a + o, 16)), device_id_type=MESH)

    @pl.loop(1, 32)
    def _(o):
        pl.semaphore_signal(barrier, inc=1, device_id=group(lax.rem(me_b + o, 32)), device_id_type=MESH)

    for i in range(2):
        for j in range(2):
            my_pa[i, j] = jnp.full((1, 128), ap_ref[i, j], jnp.int32)
            my_pb[i, j] = jnp.full((1, 128), bp_ref[0, 2 * i + j], jnp.int32)
    pa[me_a] = my_pa[...]
    pb[me_b] = my_pb[depth]
    own = [
        pltpu.make_async_copy(a_ref.at[:, :, piece(me_a), :], a1.at[me_a], own_sem.at[0]),
        pltpu.make_async_copy(b_ref.at[0, 2 * depth, piece(row), :], b1.at[0, me_b], own_sem.at[1]),
        pltpu.make_async_copy(b_ref.at[0, 2 * depth + 1, piece(row), :], b1.at[1, me_b], own_sem.at[2]),
    ]
    for copy in own:
        copy.start()
    pl.semaphore_wait(barrier, 46)

    def copy_a(to, frm):
        return pltpu.make_async_remote_copy(
            src_ref=a_ref.at[:, :, piece(to), :], dst_ref=a1.at[frm],
            send_sem=sa.at[to], recv_sem=xa.at[frm], device_id=plane(to), device_id_type=MESH)

    def copy_pa(to, frm):
        return pltpu.make_async_remote_copy(
            src_ref=my_pa, dst_ref=pa.at[frm],
            send_sem=spa.at[to], recv_sem=xpa.at[frm], device_id=plane(to), device_id_type=MESH)

    def copy_b(c, to, frm):
        return pltpu.make_async_remote_copy(
            src_ref=b_ref.at[0, 2 * lax.div(to, 16) + c, piece(lax.rem(to, 16)), :], dst_ref=b1.at[c, frm],
            send_sem=sb.at[c, to], recv_sem=xb.at[c, frm], device_id=group(to), device_id_type=MESH)

    def copy_pb(to, frm):
        return pltpu.make_async_remote_copy(
            src_ref=my_pb.at[lax.div(to, 16)], dst_ref=pb.at[frm],
            send_sem=spb.at[to], recv_sem=xpb.at[frm], device_id=group(to), device_id_type=MESH)

    @pl.loop(1, 32)
    def _(o):
        to = lax.rem(me_b + o, 32)
        copy_pb(to, me_b).start()
        copy_b(0, to, me_b).start()

    @pl.loop(1, 16)
    def _(o):
        to = lax.rem(me_a + o, 16)
        copy_pa(to, me_a).start()
        copy_a(to, me_a).start()

    @pl.loop(1, 32)
    def _(o):
        copy_b(1, lax.rem(me_b + o, 32), me_b).start()

    zero = jnp.zeros((8, 128), jnp.int32)

    def rank(ranks, g, k, p, before):
        p = jnp.broadcast_to(p, (8, 128))
        ranks[g, k] = jnp.where(p > 0, before, -1)
        return before + p

    @pl.loop(1, 32)
    def _(o):
        frm = lax.rem(me_b + 32 - o, 32)
        copy_pb(frm, frm).wait_recv()

    def rank_b(k, carry):
        return tuple(rank(rb, g, k, pb[k, g], carry[g]) for g in range(2))

    lax.fori_loop(0, NK, rank_b, (zero, zero))

    @pl.loop(1, 16)
    def _(o):
        frm = lax.rem(me_a + 16 - o, 16)
        copy_pa(frm, frm).wait_recv()

    def rank_a(s, carry):
        for j in range(2):
            carry = tuple(rank(ra, g, 2 * s + j, pa[s, g, j], carry[g]) for g in range(2))
        return carry

    lax.fori_loop(0, 16, rank_a, (zero, zero))

    lanes = lax.broadcasted_iota(jnp.int32, (8, 128), 1)
    for g in range(2):
        def meet(k, carry, g=g):
            ours = ra[g, k]
            return tuple(jnp.where(lanes == ours, rb[c, k] + 1, carry[c]) for c in range(2))

        met = lax.fori_loop(0, NK, meet, (zero, zero))
        for c in range(2):
            match[g, c] = met[c]

    def pick(ranks, load, dst, slot):
        g, j = lax.div(slot, CAP), lax.rem(slot, CAP)
        acc = [jnp.zeros((8, 128), jnp.float32)] * 4
        for k in range(NK):
            here = ranks[g, k] == j
            acc = [jnp.where(here, load(g, k, q), acc[q]) for q in range(4)]
        for q in range(4):
            dst[slot, pl.ds(8 * (q // 2), 8), pl.ds(128 * (q % 2), 128)] = acc[q]

    def tile(q):
        return pl.ds(8 * (q // 2), 8), pl.ds(128 * (q % 2), 128)

    puts = {}

    def pack_a():
        @pl.loop(1, 16)
        def _(o):
            frm = lax.rem(me_a + 16 - o, 16)
            copy_a(frm, frm).wait_recv()

        own[0].wait()

        @pl.loop(0, NSLOT)
        def _(slot):
            pick(ra, lambda g, k, q: a1[(k // 2, g, k % 2, *tile(q))], a2, slot)

        put = pltpu.make_async_copy(a2, sliced(a3, 0, NSLOT, me_a), own_sem.at[3])
        put.start()
        puts[1] = put

    def pack_b(c):
        @pl.loop(1, 32)
        def _(o):
            frm = lax.rem(me_b + 32 - o, 32)
            copy_b(c, frm, frm).wait_recv()

        own[1 + c].wait()

        @pl.loop(c * CAP, (c + 1) * CAP)
        def _(slot):
            pick(rb, lambda g, k, q: b1[(c, k, *tile(q))], b2, slot)

        put = pltpu.make_async_copy(b2.at[pl.ds(c * CAP, CAP)], sliced(b3[c], 0, CAP, row), own_sem.at[4 + c])
        put.start()
        puts[2 * c] = put

    transfers = gather_transfers(row, col, depth, a2, b2, a3, b3)
    assert len(transfers) == NXFER
    made = {}
    for i, (key, src, dst, dev, arrives, needs) in enumerate(transfers):
        made[key] = tuple(
            pltpu.make_async_remote_copy(src_ref=a, dst_ref=b, send_sem=ring_s.at[i], recv_sem=ring_x.at[i],
                                         device_id=dev, device_id_type=MESH)
            for a, b in ((src, dst), (arrives, arrives)))
    arrived = set()

    def wait_for(keys):
        for key in keys:
            if key not in arrived:
                made[key][1].wait_recv()
                arrived.add(key)

    smem_copy = pltpu.make_async_copy(match, match_s, own_sem.at[6])
    smem_copy.start()
    def split(x):
        high = x.astype(jnp.bfloat16)
        return high, (x - high.astype(jnp.float32)).astype(jnp.bfloat16)

    def block(g, c, dst):
        dst[c] = jnp.zeros((BS, BS), jnp.float32)

        @pl.loop(0, CAP)
        def _(j):
            slot = match_s[g, c, 0, j]
            weight = jnp.where(slot > 0, 1.0, 0.0).astype(jnp.float32)
            ah, al = split(a3[g * CAP + j])
            bh, bl = split(b3[c][jnp.maximum(slot - 1, 0)])
            left = jnp.concatenate([ah, ah, al], axis=1)
            right = jnp.concatenate([bh, bl, bh], axis=0)
            dst[c] += weight * jnp.dot(left, right, preferred_element_type=jnp.float32)

    other = device(row, col, 1 - depth)

    def swap(c, d):
        return pltpu.make_async_remote_copy(src_ref=c_other.at[c], dst_ref=out.at[2 * d + c], send_sem=swap_s.at[c],
                                            recv_sem=swap_x.at[c], device_id=other, device_id_type=MESH)

    keeps = []

    def start(t):
        wait_for(t[5])
        made[t[0]][0].start()

    def column_other(c):
        wait_for([t[0] for t in transfers if t[0][0] == "A" or B_CHUNKS[t[0][1]][0] == c])
        if c == 0:
            puts[1].wait()
            smem_copy.wait()
        puts[2 * c].wait()
        block(1 - depth, c, c_other)
        swap(c, depth).start()

    def column_own(c):
        block(depth, c, c_own)
        keep = pltpu.make_async_copy(c_own.at[c], out.at[2 * depth + c], own_sem.at[7 + c])
        keep.start()
        keeps.append(keep)

    actions = [(start_time(t[0]), functools.partial(start, t)) for t in transfers]
    actions += [
        (35.9, lambda: pack_b(0)), (38.4, pack_a), (44.9, lambda: pack_b(1)),
        (65.4, lambda: column_other(0)), (68.4, lambda: column_own(0)),
        (100, lambda: column_other(1)), (101, lambda: column_own(1)),
    ]
    for _, action in sorted(actions, key=lambda t: t[0]):
        action()

    for t in transfers:
        made[t[0]][0].wait_send()

    @pl.loop(1, 32)
    def _(o):
        to = lax.rem(me_b + o, 32)
        copy_pb(to, me_b).wait_send()
        copy_b(0, to, me_b).wait_send()
        copy_b(1, to, me_b).wait_send()

    @pl.loop(1, 16)
    def _(o):
        to = lax.rem(me_a + o, 16)
        copy_pa(to, me_a).wait_send()
        copy_a(to, me_a).wait_send()

    for c in range(2):
        keeps[c].wait()
        swap(c, 1 - depth).wait_recv()
        swap(c, depth).wait_send()


def multiply(a_pattern, b_pattern, a_blocks, b_blocks):
    any_spec = pl.BlockSpec(memory_space=pl.ANY)
    smem = pl.BlockSpec(memory_space=pltpu.SMEM)
    dma = pltpu.SemaphoreType.DMA
    f32, i32 = jnp.float32, jnp.int32
    return pl.pallas_call(
        kernel,
        out_shape=jax.ShapeDtypeStruct((4, BS, BS), f32),
        in_specs=[smem, smem, any_spec, any_spec],
        out_specs=any_spec,
        scratch_shapes=[
            pltpu.VMEM((16, 2, 2, SL, BS), f32), pltpu.VMEM((2, NK, SL, BS), f32),
            pltpu.VMEM((16, 2, 2, 1, 128), i32), pltpu.VMEM((NK, 2, 1, 128), i32),
            pltpu.VMEM((2, 2, 1, 128), i32), pltpu.VMEM((2, 2, 1, 128), i32),
            pltpu.VMEM((2, NK, 8, 128), i32), pltpu.VMEM((2, NK, 8, 128), i32),
            pltpu.VMEM((NSLOT, SL, BS), f32), pltpu.VMEM((NSLOT, SL, BS), f32),
            pltpu.VMEM((NSLOT, BS, BS), f32), pltpu.VMEM((CAP, BS, BS), f32), pltpu.VMEM((CAP, BS, BS), f32),
            pltpu.VMEM((2, BS, BS), f32), pltpu.VMEM((2, BS, BS), f32),
            pltpu.VMEM((2, 2, 8, 128), i32), pltpu.SMEM((2, 2, 8, 128), i32),
            dma((16,)), dma((16,)), dma((16,)), dma((16,)),
            dma((2, 32)), dma((2, 32)), dma((32,)), dma((32,)),
            dma((9,)), dma((NXFER,)), dma((NXFER,)), dma((2,)), dma((2,)),
        ],
        compiler_params=pltpu.CompilerParams(collective_id=0, has_side_effects=True),
        name="multiply",
    )(a_pattern, b_pattern, a_blocks, b_blocks)


def local(a_blocks, a_pattern, b_blocks, b_pattern, c_pattern):
    c = multiply(a_pattern, b_pattern, a_blocks, b_blocks)
    return (c * c_pattern[0][:, None, None].astype(jnp.float32))[None]


def solution(mesh):
    in_specs = (
        P("row", ("depth", "col"), None, None),
        P("row", ("depth", "col")),
        P(("depth", "row"), "col", None, None),
        P(("depth", "row"), "col"),
        P(("row", "depth"), "col"),
    )
    out_specs = P(("row", "depth"), "col", None, None)
    return jax.shard_map(local, mesh=mesh, in_specs=in_specs, out_specs=out_specs, check_vma=False)
```

```python
import functools

import jax
import jax.numpy as jnp
from jax import lax
from jax.experimental import pallas as pl
from jax.experimental.pallas import tpu as pltpu
from jax.sharding import PartitionSpec as P

MESH = pl.DeviceIdType.MESH
BS = 256
SL = 16
CAP = 8
NSLOT = 2 * CAP
NK = 32
A_CHUNKS = ((0, 8, "yx"), (8, 8, "xy"))
B_CHUNKS = ((0, 0, 4, 1), (0, 4, 4, -1), (1, 0, 4, 1), (1, 4, 4, -1))
NXFER = 20 * len(A_CHUNKS) + 15 * len(B_CHUNKS)


def device(row, col, depth):
    return {"row": row, "col": col, "depth": depth}


def sliced(ref, first, count, piece):
    return ref.at[pl.ds(first, count), pl.ds(pl.multiple_of(piece * SL, SL), SL), :]


def gather_transfers(row, col, depth, a2, b2, a3, b3):
    z, core = lax.div(row, 2), lax.rem(row, 2)
    px = lax.rem(col, 4)
    py = lax.div(col, 4) * 2 + depth

    def plane_id(x, y):
        return lax.rem(y, 2) * 8 + lax.div(y, 2) * 4 + x

    def moved(chunk, first, second):
        dx, dy = (first, second) if A_CHUNKS[chunk][2] == "xy" else (second, first)
        return lax.rem(px + (dx + 4), 4), lax.rem(py + (dy + 4), 4)

    def plane_device(chunk, first, second):
        x, y = moved(chunk, first, second)
        return device(row, lax.div(y, 2) * 4 + x, lax.rem(y, 2))

    out = []

    def a_piece(chunk, first, second, lo, count):
        if first == 0 and second == 0:
            return a2.at[pl.ds(lo, count)]
        return sliced(a3, lo, count, plane_id(*moved(chunk, first, second)))

    def a_target(chunk, first, second, lo, count):
        return sliced(a3, lo, count, plane_id(*moved(chunk, first, second)))

    for chunk in range(len(A_CHUNKS)):
        lo, count, _ = A_CHUNKS[chunk]
        half = {1: lo, -1: lo + count // 2}
        for way in (1, -1):
            key = ("A", chunk, 1, way)
            out.append((key, a_piece(chunk, 0, 0, lo, count), a_target(chunk, 0, 0, lo, count),
                        plane_device(chunk, way, 0), a_target(chunk, -way, 0, lo, count), []))
            out.append((("A", chunk, "1h", way), a_piece(chunk, -way, 0, half[way], count // 2),
                        a_target(chunk, -way, 0, half[way], count // 2), plane_device(chunk, way, 0),
                        a_target(chunk, 2, 0, half[way], count // 2), [key]))
        for first in (0, -1, 1, 2):
            needs = {0: [], -1: [("A", chunk, 1, 1)], 1: [("A", chunk, 1, -1)],
                     2: [("A", chunk, "1h", 1), ("A", chunk, "1h", -1)]}[first]
            for way in (1, -1):
                key = ("A", chunk, 2, first, way)
                out.append((key, a_piece(chunk, first, 0, lo, count), a_target(chunk, first, 0, lo, count),
                            plane_device(chunk, 0, way), a_target(chunk, first, -way, lo, count), needs))
                out.append((("A", chunk, "2h", first, way), a_piece(chunk, first, -way, half[way], count // 2),
                            a_target(chunk, first, -way, half[way], count // 2), plane_device(chunk, 0, way),
                            a_target(chunk, first, 2, half[way], count // 2), [key]))

    def b_id(dz, which):
        return lax.rem(z + (dz + 8), 8) * 2 + which

    def b_piece(chunk, dz):
        c, lo, count, _ = B_CHUNKS[chunk]
        if dz == 0:
            return b2.at[pl.ds(c * CAP + lo, count)]
        return sliced(b3[c], lo, count, b_id(dz, core))

    def b_target(chunk, dz, which):
        c, lo, count, _ = B_CHUNKS[chunk]
        return sliced(b3[c], lo, count, b_id(dz, which))

    for chunk in range(len(B_CHUNKS)):
        arrived = {0: []}
        for way in (1, -1):
            for hop in range(4):
                if hop == 3 and way != B_CHUNKS[chunk][3]:
                    continue
                key = ("B", chunk, way, hop)
                out.append((key, b_piece(chunk, -way * hop), b_target(chunk, -way * hop, core),
                            device(b_id(way, core), col, depth), b_target(chunk, -way * (hop + 1), core),
                            [("B", chunk, way, hop - 1)] if hop else []))
                arrived[-way * (hop + 1)] = [key]
        for dz, needs in arrived.items():
            out.append((("S", chunk, dz), b_piece(chunk, dz), b_target(chunk, dz, core),
                        device(z * 2 + 1 - core, col, depth), b_target(chunk, dz, 1 - core), needs))
    return out


def start_time(key):
    if key[0] == "A":
        level = {1: 0, "1h": 1}.get(key[2])
        if level is None:
            level = {0: 0, -1: 1, 1: 1, 2: 2}[key[3]] + (1 if key[2] == "2h" else 0)
        return (39.6, 46.3, 54.8, 66.5)[level] + 0.3 * key[1]
    c, lo = B_CHUNKS[key[1]][:2]
    times = ((36.8, 43.4, 49.2, 55.6), (44.1, 50.2, 54.7, 64.8))[c]
    if key[0] == "B":
        return times[key[3]] + 1.3 * lo / 4
    return times[min(abs(key[2]), 3)] + 1.3 * lo / 4 + (0.1 if abs(key[2]) < 4 else 4.5)


def kernel(ap_ref, bp_ref, a_ref, b_ref, out,
           a1, b1, pa, pb, my_pa, my_pb, ra, rb, a2, b2, a3, b3_0, b3_1, c_own, c_other, match, match_s,
           sa, xa, spa, xpa, sb, xb, spb, xpb, own_sem, ring_s, ring_x, swap_s, swap_x):
    row, col, depth = lax.axis_index("row"), lax.axis_index("col"), lax.axis_index("depth")
    b3 = (b3_0, b3_1)
    me_a = depth * 8 + col
    me_b = depth * 16 + row

    def plane(i):
        return device(row, lax.rem(i, 8), lax.div(i, 8))

    def group(i):
        return device(lax.rem(i, 16), col, lax.div(i, 16))

    def piece(i):
        return pl.ds(pl.multiple_of(i * SL, SL), SL)

    barrier = pltpu.get_barrier_semaphore()

    @pl.loop(1, 16)
    def _(o):
        pl.semaphore_signal(barrier, inc=1, device_id=plane(lax.rem(me_a + o, 16)), device_id_type=MESH)

    @pl.loop(1, 32)
    def _(o):
        pl.semaphore_signal(barrier, inc=1, device_id=group(lax.rem(me_b + o, 32)), device_id_type=MESH)

    for i in range(2):
        for j in range(2):
            my_pa[i, j] = jnp.full((1, 128), ap_ref[i, j], jnp.int32)
            my_pb[i, j] = jnp.full((1, 128), bp_ref[0, 2 * i + j], jnp.int32)
    pa[me_a] = my_pa[...]
    pb[me_b] = my_pb[depth]
    own = [
        pltpu.make_async_copy(a_ref.at[:, :, piece(me_a), :], a1.at[me_a], own_sem.at[0]),
        pltpu.make_async_copy(b_ref.at[0, 2 * depth, piece(row), :], b1.at[0, me_b], own_sem.at[1]),
        pltpu.make_async_copy(b_ref.at[0, 2 * depth + 1, piece(row), :], b1.at[1, me_b], own_sem.at[2]),
    ]
    for copy in own:
        copy.start()
    pl.semaphore_wait(barrier, 46)

    def copy_a(to, frm):
        return pltpu.make_async_remote_copy(
            src_ref=a_ref.at[:, :, piece(to), :], dst_ref=a1.at[frm],
            send_sem=sa.at[to], recv_sem=xa.at[frm], device_id=plane(to), device_id_type=MESH)

    def copy_pa(to, frm):
        return pltpu.make_async_remote_copy(
            src_ref=my_pa, dst_ref=pa.at[frm],
            send_sem=spa.at[to], recv_sem=xpa.at[frm], device_id=plane(to), device_id_type=MESH)

    def copy_b(c, to, frm):
        return pltpu.make_async_remote_copy(
            src_ref=b_ref.at[0, 2 * lax.div(to, 16) + c, piece(lax.rem(to, 16)), :], dst_ref=b1.at[c, frm],
            send_sem=sb.at[c, to], recv_sem=xb.at[c, frm], device_id=group(to), device_id_type=MESH)

    def copy_pb(to, frm):
        return pltpu.make_async_remote_copy(
            src_ref=my_pb.at[lax.div(to, 16)], dst_ref=pb.at[frm],
            send_sem=spb.at[to], recv_sem=xpb.at[frm], device_id=group(to), device_id_type=MESH)

    def far_first(t):
        step = lax.div(t + 1, 2)
        return 8 + step * (2 * lax.rem(t, 2) - 1)

    def each_b(send):
        @pl.loop(0, 15)
        def _(t):
            there = lax.rem(row + far_first(t), 16)
            send((1 - depth) * 16 + there)
            send(depth * 16 + there)

        send((1 - depth) * 16 + row)

    def send_first(to):
        copy_pb(to, me_b).start()
        copy_b(0, to, me_b).start()

    each_b(send_first)

    @pl.loop(1, 16)
    def _(o):
        to = lax.rem(me_a + o, 16)
        copy_pa(to, me_a).start()
        copy_a(to, me_a).start()

    each_b(lambda to: copy_b(1, to, me_b).start())

    zero = jnp.zeros((8, 128), jnp.int32)

    def rank(ranks, g, k, p, before):
        p = jnp.broadcast_to(p, (8, 128))
        ranks[g, k] = jnp.where(p > 0, before, -1)
        return before + p

    @pl.loop(1, 32)
    def _(o):
        frm = lax.rem(me_b + 32 - o, 32)
        copy_pb(frm, frm).wait_recv()

    def rank_b(k, carry):
        return tuple(rank(rb, g, k, pb[k, g], carry[g]) for g in range(2))

    lax.fori_loop(0, NK, rank_b, (zero, zero))

    @pl.loop(1, 16)
    def _(o):
        frm = lax.rem(me_a + 16 - o, 16)
        copy_pa(frm, frm).wait_recv()

    def rank_a(s, carry):
        for j in range(2):
            carry = tuple(rank(ra, g, 2 * s + j, pa[s, g, j], carry[g]) for g in range(2))
        return carry

    lax.fori_loop(0, 16, rank_a, (zero, zero))

    lanes = lax.broadcasted_iota(jnp.int32, (8, 128), 1)
    for g in range(2):
        def meet(k, carry, g=g):
            ours = ra[g, k]
            return tuple(jnp.where(lanes == ours, rb[c, k] + 1, carry[c]) for c in range(2))

        met = lax.fori_loop(0, NK, meet, (zero, zero))
        for c in range(2):
            match[g, c] = met[c]

    def pick(ranks, load, dst, slot):
        g, j = lax.div(slot, CAP), lax.rem(slot, CAP)
        acc = [jnp.zeros((8, 128), jnp.float32)] * 4
        for k in range(NK):
            here = ranks[g, k] == j
            acc = [jnp.where(here, load(g, k, q), acc[q]) for q in range(4)]
        for q in range(4):
            dst[slot, pl.ds(8 * (q // 2), 8), pl.ds(128 * (q % 2), 128)] = acc[q]

    def tile(q):
        return pl.ds(8 * (q // 2), 8), pl.ds(128 * (q % 2), 128)

    puts = {}

    def pack_a():
        @pl.loop(1, 16)
        def _(o):
            frm = lax.rem(me_a + 16 - o, 16)
            copy_a(frm, frm).wait_recv()

        own[0].wait()

        @pl.loop(0, NSLOT)
        def _(slot):
            pick(ra, lambda g, k, q: a1[(k // 2, g, k % 2, *tile(q))], a2, slot)

        put = pltpu.make_async_copy(a2, sliced(a3, 0, NSLOT, me_a), own_sem.at[3])
        put.start()
        puts[1] = put

    def pack_b(c):
        @pl.loop(1, 32)
        def _(o):
            frm = lax.rem(me_b + 32 - o, 32)
            copy_b(c, frm, frm).wait_recv()

        own[1 + c].wait()

        @pl.loop(c * CAP, (c + 1) * CAP)
        def _(slot):
            pick(rb, lambda g, k, q: b1[(c, k, *tile(q))], b2, slot)

        put = pltpu.make_async_copy(b2.at[pl.ds(c * CAP, CAP)], sliced(b3[c], 0, CAP, row), own_sem.at[4 + c])
        put.start()
        puts[2 * c] = put

    transfers = gather_transfers(row, col, depth, a2, b2, a3, b3)
    assert len(transfers) == NXFER
    made = {}
    for i, (key, src, dst, dev, arrives, needs) in enumerate(transfers):
        made[key] = tuple(
            pltpu.make_async_remote_copy(src_ref=a, dst_ref=b, send_sem=ring_s.at[i], recv_sem=ring_x.at[i],
                                         device_id=dev, device_id_type=MESH)
            for a, b in ((src, dst), (arrives, arrives)))
    arrived = set()

    def wait_for(keys):
        for key in keys:
            if key not in arrived:
                made[key][1].wait_recv()
                arrived.add(key)

    smem_copy = pltpu.make_async_copy(match, match_s, own_sem.at[6])
    smem_copy.start()
    def split(x):
        high = x.astype(jnp.bfloat16)
        return high, (x - high.astype(jnp.float32)).astype(jnp.bfloat16)

    def block(g, c, dst):
        dst[c] = jnp.zeros((BS, BS), jnp.float32)

        @pl.loop(0, CAP)
        def _(j):
            slot = match_s[g, c, 0, j]
            weight = jnp.where(slot > 0, 1.0, 0.0).astype(jnp.float32)
            ah, al = split(a3[g * CAP + j])
            bh, bl = split(b3[c][jnp.maximum(slot - 1, 0)])
            left = jnp.concatenate([ah, ah, al], axis=1)
            right = jnp.concatenate([bh, bl, bh], axis=0)
            dst[c] += weight * jnp.dot(left, right, preferred_element_type=jnp.float32)

    other = device(row, col, 1 - depth)

    def swap(c, d):
        return pltpu.make_async_remote_copy(src_ref=c_other.at[c], dst_ref=out.at[2 * d + c], send_sem=swap_s.at[c],
                                            recv_sem=swap_x.at[c], device_id=other, device_id_type=MESH)

    keeps = []

    def start(t):
        wait_for(t[5])
        made[t[0]][0].start()

    def column_other(c):
        wait_for([t[0] for t in transfers if t[0][0] == "A" or B_CHUNKS[t[0][1]][0] == c])
        if c == 0:
            puts[1].wait()
            smem_copy.wait()
        puts[2 * c].wait()
        block(1 - depth, c, c_other)
        swap(c, depth).start()

    def column_own(c):
        block(depth, c, c_own)
        keep = pltpu.make_async_copy(c_own.at[c], out.at[2 * depth + c], own_sem.at[7 + c])
        keep.start()
        keeps.append(keep)

    actions = [(start_time(t[0]), functools.partial(start, t)) for t in transfers]
    actions += [
        (36.66, lambda: pack_b(0)), (39.51, pack_a), (43.97, lambda: pack_b(1)),
        (70.4, lambda: column_other(0)), (73.4, lambda: column_own(0)),
        (100, lambda: column_other(1)), (101, lambda: column_own(1)),
    ]
    for _, action in sorted(actions, key=lambda t: t[0]):
        action()

    for t in transfers:
        made[t[0]][0].wait_send()

    @pl.loop(1, 32)
    def _(o):
        to = lax.rem(me_b + o, 32)
        copy_pb(to, me_b).wait_send()
        copy_b(0, to, me_b).wait_send()
        copy_b(1, to, me_b).wait_send()

    @pl.loop(1, 16)
    def _(o):
        to = lax.rem(me_a + o, 16)
        copy_pa(to, me_a).wait_send()
        copy_a(to, me_a).wait_send()

    for c in range(2):
        keeps[c].wait()
        swap(c, 1 - depth).wait_recv()
        swap(c, depth).wait_send()


def multiply(a_pattern, b_pattern, a_blocks, b_blocks):
    any_spec = pl.BlockSpec(memory_space=pl.ANY)
    smem = pl.BlockSpec(memory_space=pltpu.SMEM)
    dma = pltpu.SemaphoreType.DMA
    f32, i32 = jnp.float32, jnp.int32
    return pl.pallas_call(
        kernel,
        out_shape=jax.ShapeDtypeStruct((4, BS, BS), f32),
        in_specs=[smem, smem, any_spec, any_spec],
        out_specs=any_spec,
        scratch_shapes=[
            pltpu.VMEM((16, 2, 2, SL, BS), f32), pltpu.VMEM((2, NK, SL, BS), f32),
            pltpu.VMEM((16, 2, 2, 1, 128), i32), pltpu.VMEM((NK, 2, 1, 128), i32),
            pltpu.VMEM((2, 2, 1, 128), i32), pltpu.VMEM((2, 2, 1, 128), i32),
            pltpu.VMEM((2, NK, 8, 128), i32), pltpu.VMEM((2, NK, 8, 128), i32),
            pltpu.VMEM((NSLOT, SL, BS), f32), pltpu.VMEM((NSLOT, SL, BS), f32),
            pltpu.VMEM((NSLOT, BS, BS), f32), pltpu.VMEM((CAP, BS, BS), f32), pltpu.VMEM((CAP, BS, BS), f32),
            pltpu.VMEM((2, BS, BS), f32), pltpu.VMEM((2, BS, BS), f32),
            pltpu.VMEM((2, 2, 8, 128), i32), pltpu.SMEM((2, 2, 8, 128), i32),
            dma((16,)), dma((16,)), dma((16,)), dma((16,)),
            dma((2, 32)), dma((2, 32)), dma((32,)), dma((32,)),
            dma((9,)), dma((NXFER,)), dma((NXFER,)), dma((2,)), dma((2,)),
        ],
        compiler_params=pltpu.CompilerParams(collective_id=0, has_side_effects=True),
        name="multiply",
    )(a_pattern, b_pattern, a_blocks, b_blocks)


def local(a_blocks, a_pattern, b_blocks, b_pattern, c_pattern):
    c = multiply(a_pattern, b_pattern, a_blocks, b_blocks)
    return (c * c_pattern[0][:, None, None].astype(jnp.float32))[None]


def solution(mesh):
    in_specs = (
        P("row", ("depth", "col"), None, None),
        P("row", ("depth", "col")),
        P(("depth", "row"), "col", None, None),
        P(("depth", "row"), "col"),
        P(("row", "depth"), "col"),
    )
    out_specs = P(("row", "depth"), "col", None, None)
    return jax.shard_map(local, mesh=mesh, in_specs=in_specs, out_specs=out_specs, check_vma=False)
```

```python
import functools

import jax
import jax.numpy as jnp
from jax import lax
from jax.experimental import pallas as pl
from jax.experimental.pallas import tpu as pltpu
from jax.sharding import PartitionSpec as P

MESH = pl.DeviceIdType.MESH
BS = 256
SL = 16
CAP = 8
NSLOT = 2 * CAP
NK = 32
A_CHUNKS = ((0, 8, "yx"), (8, 8, "xy"))
B_CHUNKS = ((0, 0, 4, 1), (0, 4, 4, -1), (1, 0, 4, -1), (1, 4, 4, 1))
NXFER = 20 * len(A_CHUNKS) + 15 * len(B_CHUNKS)


def device(row, col, depth):
    return {"row": row, "col": col, "depth": depth}


def sliced(ref, first, count, piece):
    return ref.at[pl.ds(first, count), pl.ds(pl.multiple_of(piece * SL, SL), SL), :]


def gather_transfers(row, col, depth, a2, b2, a3, b3):
    z, core = lax.div(row, 2), lax.rem(row, 2)
    px = lax.rem(col, 4)
    py = lax.div(col, 4) * 2 + depth

    def plane_id(x, y):
        return lax.rem(y, 2) * 8 + lax.div(y, 2) * 4 + x

    def moved(chunk, first, second):
        dx, dy = (first, second) if A_CHUNKS[chunk][2] == "xy" else (second, first)
        return lax.rem(px + (dx + 4), 4), lax.rem(py + (dy + 4), 4)

    def plane_device(chunk, first, second):
        x, y = moved(chunk, first, second)
        return device(row, lax.div(y, 2) * 4 + x, lax.rem(y, 2))

    out = []

    def a_piece(chunk, first, second, lo, count):
        if first == 0 and second == 0:
            return a2.at[pl.ds(lo, count)]
        return sliced(a3, lo, count, plane_id(*moved(chunk, first, second)))

    def a_target(chunk, first, second, lo, count):
        return sliced(a3, lo, count, plane_id(*moved(chunk, first, second)))

    for chunk in range(len(A_CHUNKS)):
        lo, count, _ = A_CHUNKS[chunk]
        half = {1: lo, -1: lo + count // 2}
        for way in (1, -1):
            key = ("A", chunk, 1, way)
            out.append((key, a_piece(chunk, 0, 0, lo, count), a_target(chunk, 0, 0, lo, count),
                        plane_device(chunk, way, 0), a_target(chunk, -way, 0, lo, count), []))
            out.append((("A", chunk, "1h", way), a_piece(chunk, -way, 0, half[way], count // 2),
                        a_target(chunk, -way, 0, half[way], count // 2), plane_device(chunk, way, 0),
                        a_target(chunk, 2, 0, half[way], count // 2), [key]))
        for first in (0, -1, 1, 2):
            needs = {0: [], -1: [("A", chunk, 1, 1)], 1: [("A", chunk, 1, -1)],
                     2: [("A", chunk, "1h", 1), ("A", chunk, "1h", -1)]}[first]
            for way in (1, -1):
                key = ("A", chunk, 2, first, way)
                out.append((key, a_piece(chunk, first, 0, lo, count), a_target(chunk, first, 0, lo, count),
                            plane_device(chunk, 0, way), a_target(chunk, first, -way, lo, count), needs))
                out.append((("A", chunk, "2h", first, way), a_piece(chunk, first, -way, half[way], count // 2),
                            a_target(chunk, first, -way, half[way], count // 2), plane_device(chunk, 0, way),
                            a_target(chunk, first, 2, half[way], count // 2), [key]))

    def b_id(dz, which):
        return lax.rem(z + (dz + 8), 8) * 2 + which

    def b_piece(chunk, dz):
        c, lo, count, _ = B_CHUNKS[chunk]
        if dz == 0:
            return b2.at[pl.ds(c * CAP + lo, count)]
        return sliced(b3[c], lo, count, b_id(dz, core))

    def b_target(chunk, dz, which):
        c, lo, count, _ = B_CHUNKS[chunk]
        return sliced(b3[c], lo, count, b_id(dz, which))

    for chunk in range(len(B_CHUNKS)):
        arrived = {0: []}
        for way in (1, -1):
            for hop in range(4):
                if hop == 3 and way != B_CHUNKS[chunk][3]:
                    continue
                key = ("B", chunk, way, hop)
                out.append((key, b_piece(chunk, -way * hop), b_target(chunk, -way * hop, core),
                            device(b_id(way, core), col, depth), b_target(chunk, -way * (hop + 1), core),
                            [("B", chunk, way, hop - 1)] if hop else []))
                arrived[-way * (hop + 1)] = [key]
        for dz, needs in arrived.items():
            out.append((("S", chunk, dz), b_piece(chunk, dz), b_target(chunk, dz, core),
                        device(z * 2 + 1 - core, col, depth), b_target(chunk, dz, 1 - core), needs))
    return out


def start_time(key):
    if key[0] == "A":
        level = {1: 0, "1h": 1}.get(key[2])
        if level is None:
            level = {0: 0, -1: 1, 1: 1, 2: 2}[key[3]] + (1 if key[2] == "2h" else 0)
        return (39.6, 46.3, 54.8, 66.5)[level] + 0.3 * key[1]
    c, lo = B_CHUNKS[key[1]][:2]
    times = ((36.8, 43.4, 49.2, 55.6), (44.1, 50.2, 54.7, 64.8))[c]
    if key[0] == "B":
        return times[key[3]] + 1.3 * lo / 4
    return times[min(abs(key[2]), 3)] + 1.3 * lo / 4 + (0.1 if abs(key[2]) < 4 else 4.5)


def kernel(ap_ref, bp_ref, a_ref, b_ref, out,
           a1, b1, pa, pb, my_pa, my_pb, ra, rb, a2, b2, a3, b3_0, b3_1, c_own, c_other, match, match_s,
           sa, xa, spa, xpa, sb, xb, spb, xpb, own_sem, ring_s, ring_x, swap_s, swap_x):
    row, col, depth = lax.axis_index("row"), lax.axis_index("col"), lax.axis_index("depth")
    b3 = (b3_0, b3_1)
    me_a = depth * 8 + col
    me_b = depth * 16 + row

    def plane(i):
        return device(row, lax.rem(i, 8), lax.div(i, 8))

    def group(i):
        return device(lax.rem(i, 16), col, lax.div(i, 16))

    def piece(i):
        return pl.ds(pl.multiple_of(i * SL, SL), SL)

    barrier = pltpu.get_barrier_semaphore()

    @pl.loop(1, 16)
    def _(o):
        pl.semaphore_signal(barrier, inc=1, device_id=plane(lax.rem(me_a + o, 16)), device_id_type=MESH)

    @pl.loop(1, 32)
    def _(o):
        pl.semaphore_signal(barrier, inc=1, device_id=group(lax.rem(me_b + o, 32)), device_id_type=MESH)

    for i in range(2):
        for j in range(2):
            my_pa[i, j] = jnp.full((1, 128), ap_ref[i, j], jnp.int32)
            my_pb[i, j] = jnp.full((1, 128), bp_ref[0, 2 * i + j], jnp.int32)
    pa[me_a] = my_pa[...]
    pb[me_b] = my_pb[depth]
    own = [
        pltpu.make_async_copy(a_ref.at[:, :, piece(me_a), :], a1.at[me_a], own_sem.at[0]),
        pltpu.make_async_copy(b_ref.at[0, 2 * depth, piece(row), :], b1.at[0, me_b], own_sem.at[1]),
        pltpu.make_async_copy(b_ref.at[0, 2 * depth + 1, piece(row), :], b1.at[1, me_b], own_sem.at[2]),
    ]
    for copy in own:
        copy.start()
    pl.semaphore_wait(barrier, 46)

    def copy_a(to, frm):
        return pltpu.make_async_remote_copy(
            src_ref=a_ref.at[:, :, piece(to), :], dst_ref=a1.at[frm],
            send_sem=sa.at[to], recv_sem=xa.at[frm], device_id=plane(to), device_id_type=MESH)

    def copy_pa(to, frm):
        return pltpu.make_async_remote_copy(
            src_ref=my_pa, dst_ref=pa.at[frm],
            send_sem=spa.at[to], recv_sem=xpa.at[frm], device_id=plane(to), device_id_type=MESH)

    def copy_b(c, to, frm):
        return pltpu.make_async_remote_copy(
            src_ref=b_ref.at[0, 2 * lax.div(to, 16) + c, piece(lax.rem(to, 16)), :], dst_ref=b1.at[c, frm],
            send_sem=sb.at[c, to], recv_sem=xb.at[c, frm], device_id=group(to), device_id_type=MESH)

    def copy_pb(to, frm):
        return pltpu.make_async_remote_copy(
            src_ref=my_pb.at[lax.div(to, 16)], dst_ref=pb.at[frm],
            send_sem=spb.at[to], recv_sem=xpb.at[frm], device_id=group(to), device_id_type=MESH)

    def far_first(t):
        step = lax.div(t + 1, 2)
        return 8 + step * (2 * lax.rem(t, 2) - 1)

    def each_b(send):
        @pl.loop(0, 15)
        def _(t):
            there = lax.rem(row + far_first(t), 16)
            send((1 - depth) * 16 + there)
            send(depth * 16 + there)

        send((1 - depth) * 16 + row)

    def send_first(to):
        copy_pb(to, me_b).start()
        copy_b(0, to, me_b).start()

    each_b(send_first)

    @pl.loop(1, 16)
    def _(o):
        to = lax.rem(me_a + o, 16)
        copy_pa(to, me_a).start()
        copy_a(to, me_a).start()

    each_b(lambda to: copy_b(1, to, me_b).start())

    zero = jnp.zeros((8, 128), jnp.int32)

    def rank(ranks, g, k, p, before):
        p = jnp.broadcast_to(p, (8, 128))
        ranks[g, k] = jnp.where(p > 0, before, -1)
        return before + p

    @pl.loop(1, 32)
    def _(o):
        frm = lax.rem(me_b + 32 - o, 32)
        copy_pb(frm, frm).wait_recv()

    def rank_b(k, carry):
        return tuple(rank(rb, g, k, pb[k, g], carry[g]) for g in range(2))

    lax.fori_loop(0, NK, rank_b, (zero, zero))

    @pl.loop(1, 16)
    def _(o):
        frm = lax.rem(me_a + 16 - o, 16)
        copy_pa(frm, frm).wait_recv()

    def rank_a(s, carry):
        for j in range(2):
            carry = tuple(rank(ra, g, 2 * s + j, pa[s, g, j], carry[g]) for g in range(2))
        return carry

    lax.fori_loop(0, 16, rank_a, (zero, zero))

    lanes = lax.broadcasted_iota(jnp.int32, (8, 128), 1)
    for g in range(2):
        def meet(k, carry, g=g):
            ours = ra[g, k]
            return tuple(jnp.where(lanes == ours, rb[c, k] + 1, carry[c]) for c in range(2))

        met = lax.fori_loop(0, NK, meet, (zero, zero))
        for c in range(2):
            match[g, c] = met[c]

    def pick(ranks, load, dst, slot):
        g, j = lax.div(slot, CAP), lax.rem(slot, CAP)
        acc = [jnp.zeros((8, 128), jnp.float32)] * 4
        for k in range(NK):
            here = ranks[g, k] == j
            acc = [jnp.where(here, load(g, k, q), acc[q]) for q in range(4)]
        for q in range(4):
            dst[slot, pl.ds(8 * (q // 2), 8), pl.ds(128 * (q % 2), 128)] = acc[q]

    def tile(q):
        return pl.ds(8 * (q // 2), 8), pl.ds(128 * (q % 2), 128)

    puts = {}

    def pack_a():
        @pl.loop(1, 16)
        def _(o):
            frm = lax.rem(me_a + 16 - o, 16)
            copy_a(frm, frm).wait_recv()

        own[0].wait()

        @pl.loop(0, NSLOT)
        def _(slot):
            pick(ra, lambda g, k, q: a1[(k // 2, g, k % 2, *tile(q))], a2, slot)

        put = pltpu.make_async_copy(a2, sliced(a3, 0, NSLOT, me_a), own_sem.at[3])
        put.start()
        puts[1] = put

    def pack_b(c):
        @pl.loop(1, 32)
        def _(o):
            frm = lax.rem(me_b + 32 - o, 32)
            copy_b(c, frm, frm).wait_recv()

        own[1 + c].wait()

        @pl.loop(c * CAP, (c + 1) * CAP)
        def _(slot):
            pick(rb, lambda g, k, q: b1[(c, k, *tile(q))], b2, slot)

        put = pltpu.make_async_copy(b2.at[pl.ds(c * CAP, CAP)], sliced(b3[c], 0, CAP, row), own_sem.at[4 + c])
        put.start()
        puts[2 * c] = put

    transfers = gather_transfers(row, col, depth, a2, b2, a3, b3)
    assert len(transfers) == NXFER
    made = {}
    for i, (key, src, dst, dev, arrives, needs) in enumerate(transfers):
        made[key] = tuple(
            pltpu.make_async_remote_copy(src_ref=a, dst_ref=b, send_sem=ring_s.at[i], recv_sem=ring_x.at[i],
                                         device_id=dev, device_id_type=MESH)
            for a, b in ((src, dst), (arrives, arrives)))
    arrived = set()

    def wait_for(keys):
        for key in keys:
            if key not in arrived:
                made[key][1].wait_recv()
                arrived.add(key)

    smem_copy = pltpu.make_async_copy(match, match_s, own_sem.at[6])
    smem_copy.start()
    def split(x):
        high = x.astype(jnp.bfloat16)
        return high, (x - high.astype(jnp.float32)).astype(jnp.bfloat16)

    def block(g, c, dst):
        dst[c] = jnp.zeros((BS, BS), jnp.float32)

        @pl.loop(0, CAP)
        def _(j):
            slot = match_s[g, c, 0, j]
            weight = jnp.where(slot > 0, 1.0, 0.0).astype(jnp.float32)
            ah, al = split(a3[g * CAP + j])
            bh, bl = split(b3[c][jnp.maximum(slot - 1, 0)])
            left = jnp.concatenate([ah, ah, al], axis=1)
            right = jnp.concatenate([bh, bl, bh], axis=0)
            dst[c] += weight * jnp.dot(left, right, preferred_element_type=jnp.float32)

    other = device(row, col, 1 - depth)

    def swap(c, d):
        return pltpu.make_async_remote_copy(src_ref=c_other.at[c], dst_ref=out.at[2 * d + c], send_sem=swap_s.at[c],
                                            recv_sem=swap_x.at[c], device_id=other, device_id_type=MESH)

    keeps = []

    def start(t):
        wait_for(t[5])
        made[t[0]][0].start()

    def column_other(c):
        wait_for([t[0] for t in transfers if t[0][0] == "A" or B_CHUNKS[t[0][1]][0] == c])
        if c == 0:
            puts[1].wait()
            smem_copy.wait()
        puts[2 * c].wait()
        block(1 - depth, c, c_other)
        swap(c, depth).start()

    def column_own(c):
        block(depth, c, c_own)
        keep = pltpu.make_async_copy(c_own.at[c], out.at[2 * depth + c], own_sem.at[7 + c])
        keep.start()
        keeps.append(keep)

    actions = [(start_time(t[0]), functools.partial(start, t)) for t in transfers]
    actions += [
        (36.66, lambda: pack_b(0)), (39.51, pack_a), (43.97, lambda: pack_b(1)),
        (70.4, lambda: column_other(0)), (73.4, lambda: column_own(0)),
        (100, lambda: column_other(1)), (101, lambda: column_own(1)),
    ]
    for _, action in sorted(actions, key=lambda t: t[0]):
        action()

    for t in transfers:
        made[t[0]][0].wait_send()

    @pl.loop(1, 32)
    def _(o):
        to = lax.rem(me_b + o, 32)
        copy_pb(to, me_b).wait_send()
        copy_b(0, to, me_b).wait_send()
        copy_b(1, to, me_b).wait_send()

    @pl.loop(1, 16)
    def _(o):
        to = lax.rem(me_a + o, 16)
        copy_pa(to, me_a).wait_send()
        copy_a(to, me_a).wait_send()

    for c in range(2):
        keeps[c].wait()
        swap(c, 1 - depth).wait_recv()
        swap(c, depth).wait_send()


def multiply(a_pattern, b_pattern, a_blocks, b_blocks):
    any_spec = pl.BlockSpec(memory_space=pl.ANY)
    smem = pl.BlockSpec(memory_space=pltpu.SMEM)
    dma = pltpu.SemaphoreType.DMA
    f32, i32 = jnp.float32, jnp.int32
    return pl.pallas_call(
        kernel,
        out_shape=jax.ShapeDtypeStruct((4, BS, BS), f32),
        in_specs=[smem, smem, any_spec, any_spec],
        out_specs=any_spec,
        scratch_shapes=[
            pltpu.VMEM((16, 2, 2, SL, BS), f32), pltpu.VMEM((2, NK, SL, BS), f32),
            pltpu.VMEM((16, 2, 2, 1, 128), i32), pltpu.VMEM((NK, 2, 1, 128), i32),
            pltpu.VMEM((2, 2, 1, 128), i32), pltpu.VMEM((2, 2, 1, 128), i32),
            pltpu.VMEM((2, NK, 8, 128), i32), pltpu.VMEM((2, NK, 8, 128), i32),
            pltpu.VMEM((NSLOT, SL, BS), f32), pltpu.VMEM((NSLOT, SL, BS), f32),
            pltpu.VMEM((NSLOT, BS, BS), f32), pltpu.VMEM((CAP, BS, BS), f32), pltpu.VMEM((CAP, BS, BS), f32),
            pltpu.VMEM((2, BS, BS), f32), pltpu.VMEM((2, BS, BS), f32),
            pltpu.VMEM((2, 2, 8, 128), i32), pltpu.SMEM((2, 2, 8, 128), i32),
            dma((16,)), dma((16,)), dma((16,)), dma((16,)),
            dma((2, 32)), dma((2, 32)), dma((32,)), dma((32,)),
            dma((9,)), dma((NXFER,)), dma((NXFER,)), dma((2,)), dma((2,)),
        ],
        compiler_params=pltpu.CompilerParams(collective_id=0, has_side_effects=True),
        name="multiply",
    )(a_pattern, b_pattern, a_blocks, b_blocks)


def local(a_blocks, a_pattern, b_blocks, b_pattern, c_pattern):
    c = multiply(a_pattern, b_pattern, a_blocks, b_blocks)
    return (c * c_pattern[0][:, None, None].astype(jnp.float32))[None]


def solution(mesh):
    in_specs = (
        P("row", ("depth", "col"), None, None),
        P("row", ("depth", "col")),
        P(("depth", "row"), "col", None, None),
        P(("depth", "row"), "col"),
        P(("row", "depth"), "col"),
    )
    out_specs = P(("row", "depth"), "col", None, None)
    return jax.shard_map(local, mesh=mesh, in_specs=in_specs, out_specs=out_specs, check_vma=False)
```
